32 devices in a mesh: gx: 4 (over y, core), gy: 8 (over z, x).
Axes of the slice: x: 2, y: 2, z: 4, core: 2. Of those that a mesh axis runs over, the one named last changes fastest.
Arguments:
- forcing: float32 [2, 20, 64, 1024], P(None, None, 'gx', 'gy'), may hold values from -6 to 6
- viscosity: float32 [20, 64, 1024], P(None, 'gx', 'gy'), may hold values from 0.5 to 8
- spread: float32 [20, 64, 1024], P(None, 'gx', 'gy'), may hold values from 0.2 to 2
- coupling: float32 [64, 1024], P('gx', 'gy'), may hold values from -0.5 to 0.5
- friction: float32 [64, 1024], P('gx', 'gy'), may hold values from 0.05 to 5
- ice_mask: int32 [64, 1024], P('gx', 'gy'), may hold values 0 or 1
- aggregates: int32 [64, 1024], P('gx', 'gy'), may hold values from 0 to 127, as said below
Outputs:
- solution: float32 [2, 20, 64, 1024], P(None, None, 'gx', 'gy')
- residual: float32 [2, 20, 64, 1024], P(None, None, 'gx', 'gy')
The draws below stay inside these ranges and needn't reach their ends.
Inputs may be any that keep to these rules, and one draw needn't show every extreme that they name: `aggregates`: within each device block of 16 x 128 columns, every number from 0 to 127 names some columns of that block.
All inputs are finite; a program needn't handle non-finite values. No bound on the sum of `ice_mask` on one device may be relied on, other than what follows from the above.
Results may differ from the reference program's by a relative error of at most 0.0013.
Values sent between devices are 32-bit elements; how exact they have to be, the bound alone decides.
A program may use at most 128 MiB of HBM per device.

```python
import math
import jax
import jax.numpy as jnp
from jax import lax

CX = 16
CY = 128
L = 20
ITERS = 3
SWEEPS = 2
CSWEEPS = 4
AGG_DEV = 128
NX = 64
NY = 1024
N_GX = 4
N_GY = 8


def draw_aggregates(key, part):
    local_rows = lax.broadcasted_iota(jnp.int32, (NX, NY), 0) % CX
    local_cols = lax.broadcasted_iota(jnp.int32, (NX, NY), 1) % CY
    move_code = jax.random.randint(key, (NX, NY), 0, 12)
    row_step = jnp.where(move_code == 0, 4, jnp.where(move_code == 1, -4, 0))
    col_step = jnp.where(move_code == 2, 4, jnp.where(move_code == 3, -4, 0))
    centre = (local_rows % 4 == 1) & (local_cols % 4 == 1)
    row_step = jnp.where(centre, 0, row_step)
    col_step = jnp.where(centre, 0, col_step)
    moved_row = jnp.clip(local_rows + row_step, 0, CX - 1)
    moved_col = jnp.clip(local_cols + col_step, 0, CY - 1)
    return (moved_row // 4 * (CY // 4) + moved_col // 4).astype(jnp.int32)


def draw_forcing(key, part):
    rough_key = jax.random.fold_in(key, 11)
    phase_key = jax.random.fold_in(key, 12)
    amp_key = jax.random.fold_in(key, 13)
    first = (lax.broadcasted_iota(jnp.float32, (NX, NY), 0) + 0.5) / NX
    second = (lax.broadcasted_iota(jnp.float32, (NX, NY), 1) + 0.5) / NY
    phases = jax.random.uniform(phase_key, (2, 2), jnp.float32, 0.0, 2.0 * math.pi)
    amounts = jax.random.uniform(amp_key, (2,), jnp.float32, 0.5, 1.0)
    shape_first = jnp.cos(2.0 * math.pi * first + phases[0, 0]) * jnp.cos(2.0 * math.pi * second + phases[0, 1])
    shape_second = jnp.cos(2.0 * math.pi * first + phases[1, 0]) * jnp.cos(4.0 * math.pi * second + phases[1, 1])
    rough = jax.random.truncated_normal(rough_key, -5.0, 5.0, (2, L, NX, NY), jnp.float32)
    smooth = jnp.stack([amounts[0] * 0.6 * (1.0 + 0.5 * shape_first), amounts[1] * 0.4 * shape_second])
    return (rough + smooth[:, None]).astype(jnp.float32)


def place_ends(drawn, rng, low, high):
    longest = drawn.shape.index(max(drawn.shape))
    spots = []
    for shift in (0, 1):
        where = [jax.random.randint(jax.random.fold_in(rng, axis), (), 0, length) for axis, length in enumerate(drawn.shape)]
        where[longest] = (where[longest] + shift) % drawn.shape[longest]
        spots.append(tuple(where))
    return drawn.at[spots[0]].set(low).at[spots[1]].set(high)


def level_of(key, extent, pieces, low, high):
    def one(position, blocks):
        heights = jax.random.uniform(jax.random.fold_in(jax.random.fold_in(key, 6), position), (blocks,), jnp.float32, low / len(pieces), high / len(pieces))
        return jnp.repeat(jnp.exp(heights), extent[position] // blocks).reshape((-1,) + (1,) * (len(extent) - position - 1))

    factor_of = one(*pieces[0])
    for cut in pieces[1:]:
        factor_of = factor_of * one(*cut)
    return factor_of


def setup_inputs(seed: int = 0) -> dict:
    splits = jax.random.split(jax.random.key(seed), 8)
    return {
        "forcing": draw_forcing(jax.random.fold_in(splits[7], 71), 0),
        "viscosity": jnp.clip(jnp.exp(math.log(8.0) - 2.7725887 * jax.random.uniform(splits[1], (L, NX, NY), jnp.float32) ** level_of(splits[1], (L, NX, NY), ((1, 4), (2, 8)), -0.2, 0.2)), 0.5, 8.0),
        "spread": jnp.clip(jnp.exp(math.log(2.0) - 2.3025851 * jax.random.uniform(splits[2], (L, NX, NY), jnp.float32) ** level_of(splits[2], (L, NX, NY), ((1, 4), (2, 8)), -0.2, 0.2)), 0.2, 2.0),
        "coupling": jnp.clip(jax.random.uniform(splits[3], (NX, NY), jnp.float32, -0.5, 0.5) * level_of(splits[3], (NX, NY), ((0, 4), (1, 8)), -0.4, 0.0), -0.5, 0.5),
        "friction": jnp.clip(jnp.exp(math.log(5.0) - 4.6051702 * jax.random.uniform(splits[4], (NX, NY), jnp.float32) ** level_of(splits[4], (NX, NY), ((0, 4), (1, 8)), -0.2, 0.2)), 0.05, 5.0),
        "ice_mask": place_ends((jax.random.randint(splits[5], (NX, NY), 0, 32) < 31).astype(jnp.int32), jax.random.fold_in(splits[5], 1), 0, 1),
        "aggregates": draw_aggregates(jax.random.fold_in(splits[7], 71), 0),
    }


LINE_WEIGHT = 0.8
POINT_WEIGHT = 0.7
COARSE_WEIGHT = 0.7

def beside_all(padded):
    return (padded[..., 2:, 1:-1], padded[..., :-2, 1:-1], padded[..., 1:-1, 2:], padded[..., 1:-1, :-2])

def fine_coefficients(viscosity, spread, coupling, friction, ice_float, mask_padded):
    east_mask, west_mask, north_mask, south_mask = beside_all(mask_padded)
    vertical = 0.5 * (viscosity[:-1] + viscosity[1:]) * ice_float
    face_total = jnp.pad(vertical, ((0, 1), (0, 0), (0, 0))) + jnp.pad(vertical, ((1, 0), (0, 0), (0, 0)))
    bottom = jnp.pad(friction[None], ((0, viscosity.shape[0] - 1), (0, 0), (0, 0)))
    diagonal = ice_float * (face_total + 4.0 * spread + bottom) + (1.0 - ice_float)
    owned_spread = spread * ice_float
    return (diagonal, vertical, owned_spread * east_mask, owned_spread * west_mask, owned_spread * north_mask, owned_spread * south_mask, bottom * coupling * ice_float)

def group_layers(level_coefs, group_size):
    diagonal, vertical, to_east, to_west, to_north, to_south, crossed = level_coefs
    group_count = diagonal.shape[0] // group_size

    def fold_layers(values):
        return values.reshape((group_count, group_size) + values.shape[1:]).sum(axis=1)
    padded = jnp.concatenate([vertical, jnp.zeros_like(diagonal[:1])], axis=0)
    blocks = padded.reshape((group_count, group_size) + padded.shape[1:])
    inner_sum = blocks[:, :group_size - 1].sum(axis=1)
    return (fold_layers(diagonal) - 2.0 * inner_sum, blocks[:-1, group_size - 1], fold_layers(to_east), fold_layers(to_west), fold_layers(to_north), fold_layers(to_south), fold_layers(crossed))

def apply_stencil(level_coefs, grid_field, padded):
    diagonal, vertical, to_east, to_west, to_north, to_south, crossed = level_coefs
    east_value, west_value, north_value, south_value = beside_all(padded)
    result = diagonal * grid_field + crossed * grid_field[::-1] - (to_east * east_value + to_west * west_value + to_north * north_value + to_south * south_value)
    if vertical.shape[0] > 0:
        upward = vertical * grid_field[:, 1:]
        downward = vertical * grid_field[:, :-1]
        result = result - (jnp.pad(upward, ((0, 0), (0, 1), (0, 0), (0, 0))) + jnp.pad(downward, ((0, 0), (1, 0), (0, 0), (0, 0))))
    return result

def line_factor(level_coefs):
    diagonal, vertical = (level_coefs[0], level_coefs[1])
    inverse = [1.0 / diagonal[0]]
    upper = []
    for layer_at in range(1, diagonal.shape[0]):
        ratio_value = -vertical[layer_at - 1] * inverse[-1]
        upper.append(ratio_value)
        inverse.append(1.0 / (diagonal[layer_at] + vertical[layer_at - 1] * ratio_value))
    return (inverse, upper, vertical)

def line_solve(factor, right_side):
    inverse, upper, vertical = factor
    layers = len(inverse)
    forward = [right_side[:, 0] * inverse[0]]
    for layer_at in range(1, layers):
        forward.append((right_side[:, layer_at] + vertical[layer_at - 1] * forward[-1]) * inverse[layer_at])
    backward = [forward[-1]]
    for layer_at in range(layers - 2, -1, -1):
        backward.append(forward[layer_at] - upper[layer_at] * backward[-1])
    return jnp.stack(backward[::-1], axis=1)

def group_sum(grid_field, group_size):
    return grid_field.reshape((2, grid_field.shape[1] // group_size, group_size) + grid_field.shape[2:]).sum(axis=2)

def expand_layers(grid_field, group_size):
    return jnp.repeat(grid_field, group_size, axis=1)

def point_diagonal(column_coefs, group_ids, group_count):
    ids_padded = jnp.pad(group_ids, 1, constant_values=-1)
    east_id, west_id, north_id, south_id = beside_all(ids_padded)
    inner_sum = jnp.where(east_id == group_ids, column_coefs[2][0], 0.0) + jnp.where(west_id == group_ids, column_coefs[3][0], 0.0) + jnp.where(north_id == group_ids, column_coefs[4][0], 0.0) + jnp.where(south_id == group_ids, column_coefs[5][0], 0.0)
    return jax.ops.segment_sum((column_coefs[0][0] - inner_sum).reshape(-1), group_ids.reshape(-1), num_segments=group_count)

def coarse_coefficients(column_coefs, blocks_first, blocks_second):
    diagonal, vertical, to_east, to_west, to_north, to_south, crossed = column_coefs

    def split_block(values):
        plane = values[0]
        return plane.reshape(blocks_first, plane.shape[0] // blocks_first, blocks_second, plane.shape[1] // blocks_second)
    east_block = split_block(to_east)
    west_block = split_block(to_west)
    north_block = split_block(to_north)
    south_block = split_block(to_south)
    inner_sum = east_block[:, :-1].sum(axis=(1, 3)) + west_block[:, 1:].sum(axis=(1, 3)) + north_block[:, :, :, :-1].sum(axis=(1, 3)) + south_block[:, :, :, 1:].sum(axis=(1, 3))
    return (split_block(diagonal).sum(axis=(1, 3)) - inner_sum, split_block(crossed).sum(axis=(1, 3)), east_block[:, -1].sum(axis=2), west_block[:, 0].sum(axis=2), north_block[:, :, :, -1].sum(axis=1), south_block[:, :, :, 0].sum(axis=1))

def coarse_apply(block_table, grid_field, padded):
    diagonal, crossed, to_east, to_west, to_north, to_south = block_table
    east_value, west_value, north_value, south_value = beside_all(padded)
    return diagonal * grid_field + crossed * grid_field[::-1] - (to_east * east_value + to_west * west_value + to_north * north_value + to_south * south_value)

def coarse_jacobi(block_table, right_side, widen_rim):
    answer = COARSE_WEIGHT * right_side / block_table[0]
    for sweep_at in range(CSWEEPS - 1):
        answer = answer + COARSE_WEIGHT * (right_side - coarse_apply(block_table, answer, widen_rim(answer))) / block_table[0]
    return answer

def least_squares(columns, initial_norm):
    steps_count = len(columns)
    matrix_rows = [[columns[column_at][row_at] for column_at in range(steps_count)] for row_at in range(steps_count + 1)]
    target = [initial_norm] + [jnp.zeros_like(initial_norm) for row_at in range(steps_count)]
    for pivot_at in range(steps_count):
        top_value = matrix_rows[pivot_at][pivot_at]
        low_value = matrix_rows[pivot_at + 1][pivot_at]
        radius = jnp.sqrt(top_value * top_value + low_value * low_value)
        cosine = top_value / radius
        sine_value = low_value / radius
        for column_at in range(pivot_at, steps_count):
            upper_entry = matrix_rows[pivot_at][column_at]
            lower_entry = matrix_rows[pivot_at + 1][column_at]
            matrix_rows[pivot_at][column_at] = cosine * upper_entry + sine_value * lower_entry
            matrix_rows[pivot_at + 1][column_at] = cosine * lower_entry - sine_value * upper_entry
        upper_entry = target[pivot_at]
        lower_entry = target[pivot_at + 1]
        target[pivot_at] = cosine * upper_entry + sine_value * lower_entry
        target[pivot_at + 1] = cosine * lower_entry - sine_value * upper_entry
    weights = [None] * steps_count
    for pivot_at in reversed(range(steps_count)):
        partial_sum = target[pivot_at]
        for column_at in range(pivot_at + 1, steps_count):
            partial_sum = partial_sum - matrix_rows[pivot_at][column_at] * weights[column_at]
        weights[pivot_at] = partial_sum / matrix_rows[pivot_at][pivot_at]
    return weights

def reference(forcing, viscosity, spread, coupling, friction, ice_mask, aggregates):
    ice_float = ice_mask.astype(jnp.float32)
    fine_coefs = fine_coefficients(viscosity, spread, coupling, friction, ice_float, jnp.pad(ice_float, 1))
    middle = group_layers(fine_coefs, 2)
    column = group_layers(middle, L // 2)
    stencils = [fine_coefs, middle, column]
    factors = [line_factor(level_coefs) for level_coefs in stencils]
    device_rows = lax.broadcasted_iota(jnp.int32, (NX, NY), 0) // CX
    device_cols = lax.broadcasted_iota(jnp.int32, (NX, NY), 1) // CY
    group_ids = (aggregates + (device_rows * N_GY + device_cols) * AGG_DEV).astype(jnp.int32)
    total_groups = N_GX * N_GY * AGG_DEV
    ids_flat = group_ids.reshape(-1)
    point_diag = point_diagonal(column, group_ids, total_groups)
    block_table = coarse_coefficients(column, N_GX, N_GY)

    def apply_level(level_number, grid_field):
        padded = jnp.pad(grid_field, ((0, 0), (0, 0), (1, 1), (1, 1)))
        return apply_stencil(stencils[level_number], grid_field, padded)

    def restrict_points(grid_field):
        flattened = grid_field.reshape(2, -1)
        return jnp.stack([jax.ops.segment_sum(flattened[0], ids_flat, num_segments=total_groups), jax.ops.segment_sum(flattened[1], ids_flat, num_segments=total_groups)])

    def prolong_points(values):
        return values[:, ids_flat].reshape(2, 1, NX, NY)

    def point_apply(values):
        return restrict_points(apply_level(2, prolong_points(values)))

    def local_widen(values):
        return jnp.pad(values, ((0, 0), (1, 1), (1, 1)))

    def coarse_correction(values):
        coarse_rhs = values.reshape(2, N_GX, N_GY, AGG_DEV).sum(axis=3)
        answer = coarse_jacobi(block_table, coarse_rhs, local_widen)
        return jnp.repeat(answer.reshape(2, -1), AGG_DEV, axis=1)

    def point_cycle(right_side):
        answer = POINT_WEIGHT * right_side / point_diag
        for sweep_at in range(SWEEPS - 1):
            answer = answer + POINT_WEIGHT * (right_side - point_apply(answer)) / point_diag
        answer = answer + coarse_correction(right_side - point_apply(answer))
        for sweep_at in range(SWEEPS):
            answer = answer + POINT_WEIGHT * (right_side - point_apply(answer)) / point_diag
        return answer

    def line_cycle(level_number, right_side):
        factor = factors[level_number]
        answer = LINE_WEIGHT * line_solve(factor, right_side)
        for sweep_at in range(SWEEPS - 1):
            answer = answer + LINE_WEIGHT * line_solve(factor, right_side - apply_level(level_number, answer))
        leftover = right_side - apply_level(level_number, answer)
        if level_number == 0:
            answer = answer + expand_layers(line_cycle(1, group_sum(leftover, 2)), 2)
        elif level_number == 1:
            depth_count = leftover.shape[1]
            answer = answer + expand_layers(line_cycle(2, group_sum(leftover, depth_count)), depth_count)
        else:
            answer = answer + prolong_points(point_cycle(restrict_points(leftover)))
        for sweep_at in range(SWEEPS):
            answer = answer + LINE_WEIGHT * line_solve(factor, right_side - apply_level(level_number, answer))
        return answer
    initial_norm = jnp.sqrt(jnp.sum(forcing * forcing))
    basis = [forcing / initial_norm]
    stored = []
    columns = []
    for step_at in range(ITERS):
        search = line_cycle(0, basis[step_at])
        stored.append(search)
        image = apply_level(0, search)
        projected = [jnp.sum(vector * image) for vector in basis]
        for index_at in range(len(basis)):
            image = image - projected[index_at] * basis[index_at]
        height = jnp.sqrt(jnp.sum(image * image))
        columns.append(projected + [height] + [jnp.zeros_like(height) for row_at in range(ITERS - 1 - step_at)])
        if step_at + 1 < ITERS:
            basis.append(image / height)
    weights = least_squares(columns, initial_norm)
    solution = weights[0] * stored[0]
    for index_at in range(1, ITERS):
        solution = solution + weights[index_at] * stored[index_at]
    residual = forcing - apply_level(0, solution)
    return (solution, residual)
```

```python
import jax
import jax.numpy as jnp
from jax import lax
from jax.experimental import pallas as pl
from jax.experimental.pallas import tpu as pltpu
from jax.sharding import PartitionSpec as P

ITERS = 3
CSWEEPS = 4
LINE_WEIGHT = 0.8
POINT_WEIGHT = 0.7
COARSE_WEIGHT = 0.7
MESH = pl.DeviceIdType.MESH
F32 = jnp.float32
BF16 = jnp.bfloat16
TOP = 8


def split(x):
    high = x.astype(BF16)
    return high, (x - high.astype(F32)).astype(BF16)


def dot(a, b, ca, cb):
    return lax.dot_general(a, b, (((ca,), (cb,)), ((), ())), preferred_element_type=F32)


def total(x):
    return jnp.sum(jnp.sum(x, axis=1, keepdims=True), axis=0, keepdims=True)


def kernel(nx, ny, layers, cx, cy, forcing, viscosity, spread, coupling, friction, mask, aggs,
           solution, residual, *scratch):
    count = nx * ny
    gx = lax.axis_index("gx")
    gy = lax.axis_index("gy")
    me = gx * ny + gy
    (levels, (basis, stored, images), (hit, big_hi, big_lo, point_diag, point_cross),
     (x_out, x_in, x_send, x_recv), gathers, heights) = scratch
    lane = lax.broadcasted_iota(jnp.int32, (cx, cy), 1)
    row = lax.broadcasted_iota(jnp.int32, (cx, cy), 0)
    first_lane, last_lane, even = lane == 0, lane == cy - 1, lane % 2 == 0
    pair = lane // 2
    own = pl.ds(TOP, cx)

    sides = (
        (gx < nx - 1, (gx + 1, gy)),
        (gx > 0, (gx - 1, gy)),
        (gy < ny - 1, (gx, gy + 1)),
        (gy > 0, (gx, gy - 1)),
    )

    def swap_edges(copies):
        for d in range(4):
            pl.when(sides[d][0])(copies[d].start)
        for d in range(4):
            @pl.when(sides[d][0])
            def _():
                copies[d].wait_send()
                copies[d ^ 1].wait_recv()

    class Level:
        def __init__(self, depth, refs):
            self.depth = depth
            (self.field, self.row_out, self.row_in, self.col_out, self.col_in, self.send, self.recv,
             self.diag, self.vert, self.side, self.cross, self.inverse, self.upper,
             self.right, self.forward, self.post) = refs

        def put(self, p, k, value, packed):
            self.field[p, k, :, own, :] = value
            self.row_out[p, 0, k] = value[:, cx - 1, :]
            self.row_out[p, 1, k] = value[:, 0, :]
            for v in range(2):
                m = 2 * k + v
                packed = jnp.where(pair == m, pltpu.roll(value[v], (2 * m + 1) % cy, 1), packed)
            return packed

        def exchange(self, p, packed):
            self.col_out[p] = packed
            copies = []
            for d in range(4):
                src = self.row_out.at[p, d] if d < 2 else self.col_out.at[p]
                dst = self.row_in.at[p, d] if d < 2 else self.col_in.at[p, d - 2]
                copies.append(pltpu.make_async_remote_copy(
                    src_ref=src, dst_ref=dst, send_sem=self.send.at[p, d],
                    recv_sem=self.recv.at[p, d ^ 1], device_id=sides[d][1], device_id_type=MESH))
            swap_edges(copies)
            for k in range(self.depth):
                self.field[p, k, :, TOP - 1, :] = self.row_in[p, 0, k]
                self.field[p, k, :, TOP + cx, :] = self.row_in[p, 1, k]
            return jnp.where(even, pltpu.roll(self.col_in[p, 1], cy - 1, 1),
                             pltpu.roll(self.col_in[p, 0], 1, 1))

        def beside(self, p, k, comb):
            value = self.field[p, k, :, own, :]
            north, south = [], []
            for v in range(2):
                edge = pltpu.roll(comb, (cy - 1 - 2 * (2 * k + v)) % cy, 1)
                north.append(jnp.where(last_lane, edge, pltpu.roll(value[v], cy - 1, 1)))
                south.append(jnp.where(first_lane, edge, pltpu.roll(value[v], 1, 1)))
            return (value, self.field[p, k, :, pl.ds(TOP + 1, cx), :],
                    self.field[p, k, :, pl.ds(TOP - 1, cx), :], jnp.stack(north), jnp.stack(south))

        def sideways(self, p, k, comb):
            value, east, west, north, south = self.beside(p, k, comb)
            out = (self.side[0, k][None] * east + self.side[1, k][None] * west
                   + self.side[2, k][None] * north + self.side[3, k][None] * south)
            if k == 0:
                crossed = self.cross[...]
                out = out - jnp.stack([crossed * value[1], crossed * value[0]])
            return value, out

        def leftover(self, p, comb, right, emit):
            for k in range(self.depth):
                value, out = self.sideways(p, k, comb)
                out = out - self.diag[k][None] * value
                if k + 1 < self.depth:
                    out = out + self.vert[k][None] * self.field[p, k + 1, :, own, :]
                if k > 0:
                    out = out + self.vert[k - 1][None] * self.field[p, k - 1, :, own, :]
                emit(k, out if right is None else right(k) + out)

        def solve(self, source, old, p):
            last = None
            for k in range(self.depth):
                value = source(k)
                if k > 0:
                    value = value + self.vert[k - 1][None] * last
                last = value * self.inverse[k][None]
                self.forward[k] = last
            packed = jnp.zeros((cx, cy), F32)
            for k in reversed(range(self.depth)):
                if k + 1 < self.depth:
                    last = self.forward[k] - self.upper[k][None] * last
                value = LINE_WEIGHT * last
                if old is not None:
                    value = value + (1.0 - LINE_WEIGHT) * old(k)
                packed = self.put(p, k, value, packed)
            return packed

        def sweep(self, p, comb, right):
            return self.solve(lambda k: right(k) + self.sideways(p, k, comb)[1],
                              lambda k: self.field[p, k, :, own, :], 1 - p)

        def factor(self):
            inverse = 1.0 / self.diag[0]
            self.inverse[0] = inverse
            for k in range(1, self.depth):
                ratio = -self.vert[k - 1] * inverse
                self.upper[k - 1] = ratio
                inverse = 1.0 / (self.diag[k] + self.vert[k - 1] * ratio)
                self.inverse[k] = inverse

        def cycle(self, right, inner):
            packed = self.solve(right, None, 0)
            comb = self.exchange(0, packed)
            packed = self.sweep(0, comb, right)
            comb = self.exchange(1, packed)
            correction = inner(self, 1, comb, right)
            packed = jnp.zeros((cx, cy), F32)
            for k in range(self.depth):
                packed = self.put(0, k, self.field[1, k, :, own, :] + correction(k), packed)
            comb = self.exchange(0, packed)
            packed = self.sweep(0, comb, right)
            comb = self.exchange(1, packed)
            return self.sweep(1, comb, right)

    half = layers // 2
    fine, middle, column = (Level(n, refs) for n, refs in zip((layers, half, 1), levels))
    for d in range(4):
        @pl.when(jnp.logical_not(sides[d][0]))
        def _():
            for level in (fine, middle, column):
                for p in range(2):
                    if d < 2:
                        level.row_in[p, d ^ 1] = jnp.zeros_like(level.row_in[p, d ^ 1])
                    else:
                        level.col_in[p, (d ^ 1) - 2] = jnp.zeros((cx, cy), F32)
            for p in range(2):
                x_in[p, d] = jnp.zeros((2, cy), F32)
    basis[...] = jnp.zeros_like(basis)

    def gather(which):
        out, into, send, recv = gathers[which]

        def step(i, carry):
            target = lax.rem(me + i, count)
            pltpu.make_async_remote_copy(
                src_ref=out, dst_ref=into.at[me], send_sem=send, recv_sem=recv,
                device_id=(target // ny, lax.rem(target, ny)), device_id_type=MESH).start()
            return carry

        lax.fori_loop(1, count, step, 0)
        into[me] = out[...]
        rest = into.at[pl.ds(0, count - 1)]
        pltpu.make_async_copy(rest, rest, recv).wait()
        pltpu.make_async_copy(rest, rest, send).wait()

    wide = lax.broadcasted_iota(jnp.int32, (1, cy), 1)

    def reduce_all(parts):
        line = jnp.zeros((1, cy), F32)
        for i, part in enumerate(parts):
            line = jnp.where(wide == i, part, line)
        gathers[1][0][...] = line
        gather(1)
        return jnp.sum(gathers[1][1][:, 0, :], axis=0, keepdims=True)

    def pick(line, i):
        return jnp.sum(jnp.where(wide == i, line, 0.0), axis=1, keepdims=True)

    ice = mask[...].astype(F32)
    ids = aggs[...]
    packed = column.put(1, 0, jnp.stack([ice, ids.astype(F32)]), jnp.zeros((cx, cy), F32))
    comb = column.exchange(1, packed)
    around = column.beside(1, 0, comb)[1:]
    bottom = friction[...]
    for k in range(layers):
        faces = 4.0 * spread[k]
        if k + 1 < layers:
            face = 0.5 * (viscosity[k] + viscosity[k + 1]) * ice
            fine.vert[k] = face
            faces = faces + face
        if k > 0:
            faces = faces + fine.vert[k - 1]
        if k == 0:
            faces = faces + bottom
        fine.diag[k] = ice * faces + (1.0 - ice)
        owned = spread[k] * ice
        for d in range(4):
            fine.side[d, k] = owned * around[d][0]
    fine.cross[...] = bottom * coupling[...] * ice
    for finer, coarser in ((fine, middle), (middle, column)):
        size = finer.depth // coarser.depth
        for k in range(coarser.depth):
            group = range(k * size, (k + 1) * size)
            diag = sum(finer.diag[j] for j in group)
            inner_faces = sum(finer.vert[j] for j in list(group)[:-1])
            coarser.diag[k] = diag - 2.0 * inner_faces
            if k + 1 < coarser.depth:
                coarser.vert[k] = finer.vert[group[-1]]
            for d in range(4):
                coarser.side[d, k] = sum(finer.side[d, j] for j in group)
        coarser.cross[...] = finer.cross[...]
    for level in (fine, middle, column):
        level.factor()

    down = lax.broadcasted_iota(jnp.int32, (cy, cy), 0)
    across = lax.broadcasted_iota(jnp.int32, (cy, cy), 1)
    for r in range(cx):
        hit[r] = jnp.where(ids[r:r + 1, :] == down, 1.0, 0.0).astype(BF16)
    side2 = [column.side[d, 0] for d in range(4)]
    diag2, cross2 = column.diag[0], column.cross[...]
    near = jnp.zeros((cy, cy), F32)
    for r in range(cx):
        here = hit[r].astype(F32)
        term = diag2[r:r + 1, :] * here
        if r + 1 < cx:
            term = term - side2[0][r:r + 1, :] * hit[r + 1].astype(F32)
        if r > 0:
            term = term - side2[1][r:r + 1, :] * hit[r - 1].astype(F32)
        term = term - jnp.where(across < cy - 1, side2[2][r:r + 1, :], 0.0) * pltpu.roll(here, cy - 1, 1)
        term = term - jnp.where(across > 0, side2[3][r:r + 1, :], 0.0) * pltpu.roll(here, 1, 1)
        high, low = split(term)
        near = near + dot(high, hit[r], 1, 1) + dot(low, hit[r], 1, 1)
    point_diag[...] = jnp.sum(jnp.where(down == across, near, 0.0), axis=0, keepdims=True)
    tables = [near]
    ids_around = [value[1] for value in around]
    for d, r in ((0, cx - 1), (1, 0)):
        other = ids_around[d][r:r + 1, :].astype(jnp.int32)
        term = jnp.where(other == down, side2[d][r:r + 1, :], 0.0)
        high, low = split(term)
        tables.append(-(dot(high, hit[r], 1, 1) + dot(low, hit[r], 1, 1)))
    for d, q in ((2, cy - 1), (3, 0)):
        other = ids_around[d][:, q:q + 1].astype(jnp.int32)
        term = jnp.where(other == lane, side2[d][:, q:q + 1], 0.0)
        here = jnp.where(ids[:, q:q + 1] == lane, 1.0, 0.0)
        high, low = split(term)
        here = here.astype(BF16)
        tables.append(-(dot(high, here, 0, 0) + dot(low, here, 0, 0)))
    for i, table in enumerate(tables):
        high, low = split(table)
        big_hi[i] = high
        big_lo[i] = low

    tall = lax.broadcasted_iota(jnp.int32, (4 * cx, cy), 0) % cx

    def restrict_points(first, second):
        h0, l0 = split(first)
        h1, l1 = split(second)
        left = jnp.concatenate([h0, h1, l0, l1], axis=0)
        out = jnp.zeros((4 * cx, cy), F32)
        for r in range(cx):
            out = jnp.where(tall == r, dot(left, hit[r], 1, 1), out)
        parts = [jnp.sum(out[i * cx:(i + 1) * cx] + out[(i + 2) * cx:(i + 3) * cx], axis=0, keepdims=True)
                 for i in range(2)]
        return jnp.concatenate(parts, axis=0)

    point_cross[...] = restrict_points(cross2, cross2)

    inner = (diag2 - jnp.where(row < cx - 1, side2[0], 0.0) - jnp.where(row > 0, side2[1], 0.0)
             - jnp.where(lane < cy - 1, side2[2], 0.0) - jnp.where(lane > 0, side2[3], 0.0))
    entries = (inner, cross2, jnp.where(row == cx - 1, side2[0], 0.0), jnp.where(row == 0, side2[1], 0.0),
               jnp.where(last_lane, side2[2], 0.0), jnp.where(first_lane, side2[3], 0.0))
    eight = lax.broadcasted_iota(jnp.int32, (8, cy), 0)
    tile = jnp.zeros((8, cy), F32)
    for i, entry in enumerate(entries):
        tile = jnp.where(eight == i, total(entry), tile)
    gathers[2][0][...] = tile
    gather(2)
    block_row = lax.broadcasted_iota(jnp.int32, (count, cy), 0)

    def coarse_correction(left):
        sums = jnp.sum(left, axis=1, keepdims=True)
        gathers[0][0][...] = jnp.where(wide % 2 == 0, sums[0:1], sums[1:2])
        gather(0)
        right = gathers[0][1][:, 0, :]
        diag, crossed, east, west, north, south = (gathers[2][1][:, i, :] for i in range(6))
        answer = COARSE_WEIGHT * right / diag
        for _ in range(CSWEEPS - 1):
            applied = diag * answer + crossed * pltpu.roll(answer, 1, 1) - (
                east * pltpu.roll(answer, count - ny, 0) + west * pltpu.roll(answer, ny, 0)
                + north * pltpu.roll(answer, count - 1, 0) + south * pltpu.roll(answer, 1, 0))
            answer = answer + COARSE_WEIGHT * (right - applied) / diag
        found = []
        for at in (me, me + ny, me - ny, me + 1, me - 1):
            line = jnp.sum(jnp.where(block_row == at, answer, 0.0), axis=0, keepdims=True)
            found.append(jnp.concatenate([line[:, 0:1], line[:, 1:2]], axis=0))
        return found

    def point_exchange(p, x):
        x_out[p] = x
        copies = [pltpu.make_async_remote_copy(
            src_ref=x_out.at[p], dst_ref=x_in.at[p, d ^ 1], send_sem=x_send.at[p, d],
            recv_sem=x_recv.at[p, d ^ 1], device_id=sides[d][1], device_id_type=MESH) for d in range(4)]
        swap_edges(copies)
        return [x] + [x_in[p, d] for d in range(4)]

    def point_apply(xs):
        out = point_cross[...] * jnp.concatenate([xs[0][1:2], xs[0][0:1]], axis=0)
        for i, x in enumerate(xs):
            high, low = split(x)
            out = out + dot(high, big_hi[i], 1, 0) + dot(low, big_hi[i], 1, 0) + dot(high, big_lo[i], 1, 0)
        return out

    def point_cycle(right):
        scale = POINT_WEIGHT / point_diag[...]
        x = right * scale
        x = x + (right - point_apply(point_exchange(0, x))) * scale
        xs = point_exchange(1, x)
        found = coarse_correction(right - point_apply(xs))
        xs = [x + y for x, y in zip(xs, found)]
        x = xs[0] + (right - point_apply(xs)) * scale
        return x + (right - point_apply(point_exchange(0, x))) * scale

    def into_points(level, p, comb, right):
        kept = []
        level.leftover(p, comb, right, lambda k, value: kept.append(value))
        x = point_cycle(restrict_points(kept[0][0], kept[0][1]))
        spread_out = jnp.stack([
            jnp.take_along_axis(jnp.broadcast_to(x[v:v + 1], (cx, cy)), ids, axis=1,
                                mode="promise_in_bounds") for v in range(2)])
        return lambda k: spread_out

    def into_level(coarser, deeper):
        def inner(level, p, comb, right):
            size = level.depth // coarser.depth
            held = []

            def emit(k, value):
                held.append(value)
                if len(held) == size:
                    coarser.right[k // size] = sum(held)
                    held.clear()

            level.leftover(p, comb, right, emit)
            coarser.cycle(lambda k: coarser.right[k], deeper)
            return lambda k: coarser.field[0, k // size, :, own, :]
        return inner

    into_column = into_level(column, into_points)
    into_middle = into_level(middle, into_column)

    square = jnp.zeros((cx, cy), F32)
    for k in range(layers):
        square = square + forcing[0, k] * forcing[0, k] + forcing[1, k] * forcing[1, k]
    norm = jnp.sqrt(pick(reduce_all([total(square)]), 0))
    for k in range(layers):
        basis[0, k] = forcing[:, k] / norm

    def iteration(j, carry):
        packed = fine.cycle(lambda k: basis[j, k], into_middle)
        comb = fine.exchange(0, packed)
        sums = [jnp.zeros((cx, cy), F32) for _ in range(ITERS + 1)]

        def emit(k, value):
            value = -value
            images[j, k] = value
            stored[j, k] = fine.field[0, k, :, own, :]
            for i in range(ITERS):
                prod = basis[i, k] * value
                sums[i] = sums[i] + prod[0] + prod[1]
            sums[ITERS] = sums[ITERS] + value[0] * value[0] + value[1] * value[1]

        fine.leftover(0, comb, None, emit)
        line = reduce_all([total(s) for s in sums])
        projected = [pick(line, i) for i in range(ITERS)]
        height2 = pick(line, ITERS)
        for h in projected:
            height2 = height2 - h * h
        height = jnp.sqrt(height2)
        heights[j] = jnp.where(wide == ITERS, height, line)

        @pl.when(j + 1 < ITERS)
        def _():
            for k in range(layers):
                value = images[j, k]
                for i in range(ITERS):
                    value = value - projected[i] * basis[i, k]
                basis[j + 1, k] = value / height
        return carry

    lax.fori_loop(0, ITERS, iteration, 0)

    rows = [[None] * ITERS for _ in range(ITERS + 1)]
    for j in range(ITERS):
        line = heights[j]
        for i in range(ITERS + 1):
            if i <= j:
                rows[i][j] = pick(line, i)
            elif i == j + 1:
                rows[i][j] = pick(line, ITERS)
            else:
                rows[i][j] = jnp.zeros((1, 1), F32)
    target = [norm] + [jnp.zeros((1, 1), F32)] * ITERS
    for a in range(ITERS):
        high, low = rows[a][a], rows[a + 1][a]
        radius = jnp.sqrt(high * high + low * low)
        cosine, sine = high / radius, low / radius
        for c in range(a, ITERS):
            up, lo = rows[a][c], rows[a + 1][c]
            rows[a][c] = cosine * up + sine * lo
            rows[a + 1][c] = cosine * lo - sine * up
        up, lo = target[a], target[a + 1]
        target[a] = cosine * up + sine * lo
        target[a + 1] = cosine * lo - sine * up
    weights = [None] * ITERS
    for a in reversed(range(ITERS)):
        part = target[a]
        for c in range(a + 1, ITERS):
            part = part - rows[a][c] * weights[c]
        weights[a] = part / rows[a][a]
    for k in range(layers):
        out = weights[0] * stored[0, k]
        rest = forcing[:, k] - weights[0] * images[0, k]
        for j in range(1, ITERS):
            out = out + weights[j] * stored[j, k]
            rest = rest - weights[j] * images[j, k]
        solution[:, k] = out
        residual[:, k] = rest


def solution(mesh):
    nx, ny = mesh.shape["gx"], mesh.shape["gy"]
    count = nx * ny

    def body(forcing, viscosity, spread, coupling, friction, mask, aggs):
        layers, cx, cy = forcing.shape[1:]
        dma = pltpu.SemaphoreType.DMA

        def vm(*shape, dtype=F32):
            return pltpu.VMEM(shape, dtype)

        def level(n):
            return (
                vm(2, n, 2, cx + 2 * TOP, cy), vm(2, 2, n, 2, cy), vm(2, 2, n, 2, cy),
                vm(2, cx, cy), vm(2, 2, cx, cy), dma((2, 4)), dma((2, 4)),
                vm(n, cx, cy), vm(n, cx, cy), vm(4, n, cx, cy), vm(cx, cy), vm(n, cx, cy), vm(n, cx, cy),
                vm(n, 2, cx, cy), vm(n, 2, cx, cy), vm(1, cy),
            )

        scratch = (
            (level(layers), level(layers // 2), level(1)),
            tuple(vm(ITERS, layers, 2, cx, cy) for _ in range(3)),
            (vm(cx, cy, cy, dtype=BF16), vm(5, cy, cy, dtype=BF16), vm(5, cy, cy, dtype=BF16),
             vm(1, cy), vm(2, cy)),
            (vm(2, 2, cy), vm(2, 4, 2, cy), dma((2, 4)), dma((2, 4))),
            tuple((vm(n, cy), vm(count, n, cy), dma(()), dma(())) for n in (1, 1, 8)),
            vm(ITERS, 1, cy),
        )
        flat, tree = jax.tree.flatten(scratch)

        def run(*refs):
            kernel(nx, ny, layers, cx, cy, *refs[:9], *jax.tree.unflatten(tree, refs[9:]))

        shape = jax.ShapeDtypeStruct(forcing.shape, F32)
        whole = pl.BlockSpec(memory_space=pltpu.VMEM)
        return tuple(pl.pallas_call(
            run,
            out_shape=(shape, shape),
            in_specs=[whole] * 7,
            out_specs=(whole, whole),
            scratch_shapes=flat,
            compiler_params=pltpu.CompilerParams(has_side_effects=True, vmem_limit_bytes=60 * 1024 * 1024),
        )(forcing, viscosity, spread, coupling, friction, mask, aggs))

    return jax.shard_map(
        body,
        mesh=mesh,
        in_specs=(
            P(None, None, "gx", "gy"),
            P(None, "gx", "gy"),
            P(None, "gx", "gy"),
            P("gx", "gy"),
            P("gx", "gy"),
            P("gx", "gy"),
            P("gx", "gy"),
        ),
        out_specs=(P(None, None, "gx", "gy"), P(None, None, "gx", "gy")),
        check_vma=False,
    )
```

```python
import jax
import jax.numpy as jnp
from jax import lax
from jax.experimental import pallas as pl
from jax.experimental.pallas import tpu as pltpu
from jax.sharding import PartitionSpec as P

ITERS = 3
CSWEEPS = 4
LINE_WEIGHT = 0.8
POINT_WEIGHT = 0.7
COARSE_WEIGHT = 0.7
MESH = pl.DeviceIdType.MESH
F32 = jnp.float32
BF16 = jnp.bfloat16
TOP = 8


def split(x):
    high = x.astype(BF16)
    return high, (x - high.astype(F32)).astype(BF16)


def dot(a, b, ca, cb):
    return lax.dot_general(a, b, (((ca,), (cb,)), ((), ())), preferred_element_type=F32)


def total(x):
    return jnp.sum(jnp.sum(x, axis=1, keepdims=True), axis=0, keepdims=True)


def kernel(nx, ny, layers, cx, cy, forcing, viscosity, spread, coupling, friction, mask, aggs,
           solution, residual, *scratch):
    count = nx * ny
    gx = lax.axis_index("gx")
    gy = lax.axis_index("gy")
    me = gx * ny + gy
    (levels, (basis, stored), (hit, big_hi, big_lo, point_diag, point_cross),
     (x_out, x_in, x_send, x_recv), gathers) = scratch
    lane = lax.broadcasted_iota(jnp.int32, (cx, cy), 1)
    row = lax.broadcasted_iota(jnp.int32, (cx, cy), 0)
    first_lane, last_lane, even = lane == 0, lane == cy - 1, lane % 2 == 0
    pair = lane // 2
    own = pl.ds(TOP, cx)

    sides = (
        (gx < nx - 1, (gx + 1, gy)),
        (gx > 0, (gx - 1, gy)),
        (gy < ny - 1, (gx, gy + 1)),
        (gy > 0, (gx, gy - 1)),
    )

    def swap_edges(copies):
        for d in range(4):
            pl.when(sides[d][0])(copies[d].start)
        for d in range(4):
            @pl.when(sides[d][0])
            def _():
                copies[d].wait_send()
                copies[d ^ 1].wait_recv()

    class Level:
        def __init__(self, depth, refs):
            self.depth = depth
            self.turn = 0
            (self.field, self.row_out, self.row_in, self.col_out, self.col_in, self.send, self.recv,
             self.diag, self.vert, self.side, self.cross, self.inverse, self.upper,
             self.right, self.forward, self.post) = refs

        def put(self, p, k, value, packed):
            self.field[p, k, :, own, :] = value
            self.row_out[p, 0, k] = value[:, cx - 1, :]
            self.row_out[p, 1, k] = value[:, 0, :]
            for v in range(2):
                m = 2 * k + v
                packed = jnp.where(pair == m, pltpu.roll(value[v], (2 * m + 1) % cy, 1), packed)
            return packed

        def exchange(self, p, packed):
            self.col_out[p] = packed
            q = lax.rem(p + self.turn, 2)
            copies = []
            for d in range(4):
                src = self.row_out.at[p, d] if d < 2 else self.col_out.at[p]
                dst = self.row_in.at[q, d] if d < 2 else self.col_in.at[q, d - 2]
                copies.append(pltpu.make_async_remote_copy(
                    src_ref=src, dst_ref=dst, send_sem=self.send.at[p, d],
                    recv_sem=self.recv.at[q, d ^ 1], device_id=sides[d][1], device_id_type=MESH))
            swap_edges(copies)
            for k in range(self.depth):
                self.field[p, k, :, TOP - 1, :] = self.row_in[q, 0, k]
                self.field[p, k, :, TOP + cx, :] = self.row_in[q, 1, k]
            return jnp.where(even, pltpu.roll(self.col_in[q, 1], cy - 1, 1),
                             pltpu.roll(self.col_in[q, 0], 1, 1))

        def beside(self, p, k, comb):
            value = self.field[p, k, :, own, :]
            north, south = [], []
            for v in range(2):
                edge = pltpu.roll(comb, (cy - 1 - 2 * (2 * k + v)) % cy, 1)
                north.append(jnp.where(last_lane, edge, pltpu.roll(value[v], cy - 1, 1)))
                south.append(jnp.where(first_lane, edge, pltpu.roll(value[v], 1, 1)))
            return (value, self.field[p, k, :, pl.ds(TOP + 1, cx), :],
                    self.field[p, k, :, pl.ds(TOP - 1, cx), :], jnp.stack(north), jnp.stack(south))

        def sideways(self, p, k, comb):
            value, east, west, north, south = self.beside(p, k, comb)
            out = (self.side[0, k][None] * east + self.side[1, k][None] * west
                   + self.side[2, k][None] * north + self.side[3, k][None] * south)
            if k == 0:
                crossed = self.cross[...]
                out = out - jnp.stack([crossed * value[1], crossed * value[0]])
            return value, out

        def leftover(self, p, comb, right, emit):
            for k in range(self.depth):
                value, out = self.sideways(p, k, comb)
                out = out - self.diag[k][None] * value
                if k + 1 < self.depth:
                    out = out + self.vert[k][None] * self.field[p, k + 1, :, own, :]
                if k > 0:
                    out = out + self.vert[k - 1][None] * self.field[p, k - 1, :, own, :]
                emit(k, out if right is None else right(k) + out)

        def solve(self, source, old, p):
            last = None
            for k in range(self.depth):
                value = source(k)
                if k > 0:
                    value = value + self.vert[k - 1][None] * last
                last = value * self.inverse[k][None]
                self.forward[k] = last
            packed = jnp.zeros((cx, cy), F32)
            for k in reversed(range(self.depth)):
                if k + 1 < self.depth:
                    last = self.forward[k] - self.upper[k][None] * last
                value = LINE_WEIGHT * last
                if old is not None:
                    value = value + (1.0 - LINE_WEIGHT) * old(k)
                packed = self.put(p, k, value, packed)
            return packed

        def sweep(self, p, comb, right):
            return self.solve(lambda k: right(k) + self.sideways(p, k, comb)[1],
                              lambda k: self.field[p, k, :, own, :], 1 - p)

        def factor(self):
            inverse = 1.0 / self.diag[0]
            self.inverse[0] = inverse
            for k in range(1, self.depth):
                ratio = -self.vert[k - 1] * inverse
                self.upper[k - 1] = ratio
                inverse = 1.0 / (self.diag[k] + self.vert[k - 1] * ratio)
                self.inverse[k] = inverse

        def cycle(self, right, inner):
            packed = self.solve(right, None, 0)
            comb = self.exchange(0, packed)
            packed = self.sweep(0, comb, right)
            comb = self.exchange(1, packed)
            correction = inner(self, 1, comb, right)
            packed = jnp.zeros((cx, cy), F32)
            for k in range(self.depth):
                packed = self.put(0, k, self.field[1, k, :, own, :] + correction(k), packed)
            comb = self.exchange(0, packed)
            packed = self.sweep(0, comb, right)
            comb = self.exchange(1, packed)
            return self.sweep(1, comb, right)

    half = layers // 2
    fine, middle, column = (Level(n, refs) for n, refs in zip((layers, half, 1), levels))
    for d in range(4):
        @pl.when(jnp.logical_not(sides[d][0]))
        def _():
            for level in (fine, middle, column):
                for p in range(2):
                    if d < 2:
                        level.row_in[p, d ^ 1] = jnp.zeros_like(level.row_in[p, d ^ 1])
                    else:
                        level.col_in[p, (d ^ 1) - 2] = jnp.zeros((cx, cy), F32)
            for p in range(2):
                x_in[p, d] = jnp.zeros((2, cy), F32)

    def gather(which, slot=0):
        out, into, send, recv = gathers[which]
        into, recv = into.at[slot], recv.at[slot]

        def step(i, carry):
            target = lax.rem(me + i, count)
            pltpu.make_async_remote_copy(
                src_ref=out, dst_ref=into.at[me], send_sem=send, recv_sem=recv,
                device_id=(target // ny, lax.rem(target, ny)), device_id_type=MESH).start()
            return carry

        lax.fori_loop(1, count, step, 0)
        into[me] = out[...]
        rest = into.at[pl.ds(0, count - 1)]
        pltpu.make_async_copy(rest, rest, recv).wait()
        pltpu.make_async_copy(rest, rest, send).wait()

    wide = lax.broadcasted_iota(jnp.int32, (1, cy), 1)

    def reduce_all(parts):
        line = jnp.zeros((1, cy), F32)
        for i, part in enumerate(parts):
            line = jnp.where(wide == i, part, line)
        gathers[1][0][...] = line
        gather(1)
        return jnp.sum(gathers[1][1][0, :, 0, :], axis=0, keepdims=True)

    def pick(line, i):
        return jnp.sum(jnp.where(wide == i, line, 0.0), axis=1, keepdims=True)

    ice = mask[...].astype(F32)
    ids = aggs[...]
    packed = column.put(1, 0, jnp.stack([ice, ids.astype(F32)]), jnp.zeros((cx, cy), F32))
    comb = column.exchange(1, packed)
    around = column.beside(1, 0, comb)[1:]
    bottom = friction[...]
    for k in range(layers):
        faces = 4.0 * spread[k]
        if k + 1 < layers:
            face = 0.5 * (viscosity[k] + viscosity[k + 1]) * ice
            fine.vert[k] = face
            faces = faces + face
        if k > 0:
            faces = faces + fine.vert[k - 1]
        if k == 0:
            faces = faces + bottom
        fine.diag[k] = ice * faces + (1.0 - ice)
        owned = spread[k] * ice
        for d in range(4):
            fine.side[d, k] = owned * around[d][0]
    fine.cross[...] = bottom * coupling[...] * ice
    for finer, coarser in ((fine, middle), (middle, column)):
        size = finer.depth // coarser.depth
        for k in range(coarser.depth):
            group = range(k * size, (k + 1) * size)
            diag = sum(finer.diag[j] for j in group)
            inner_faces = sum(finer.vert[j] for j in list(group)[:-1])
            coarser.diag[k] = diag - 2.0 * inner_faces
            if k + 1 < coarser.depth:
                coarser.vert[k] = finer.vert[group[-1]]
            for d in range(4):
                coarser.side[d, k] = sum(finer.side[d, j] for j in group)
        coarser.cross[...] = finer.cross[...]
    for level in (fine, middle, column):
        level.factor()

    down = lax.broadcasted_iota(jnp.int32, (cy, cy), 0)
    across = lax.broadcasted_iota(jnp.int32, (cy, cy), 1)
    for r in range(cx):
        hit[r] = jnp.where(ids[r:r + 1, :] == down, 1.0, 0.0).astype(BF16)
    side2 = [column.side[d, 0] for d in range(4)]
    diag2, cross2 = column.diag[0], column.cross[...]
    near = jnp.zeros((cy, cy), F32)
    for r in range(cx):
        here = hit[r].astype(F32)
        term = diag2[r:r + 1, :] * here
        if r + 1 < cx:
            term = term - side2[0][r:r + 1, :] * hit[r + 1].astype(F32)
        if r > 0:
            term = term - side2[1][r:r + 1, :] * hit[r - 1].astype(F32)
        term = term - jnp.where(across < cy - 1, side2[2][r:r + 1, :], 0.0) * pltpu.roll(here, cy - 1, 1)
        term = term - jnp.where(across > 0, side2[3][r:r + 1, :], 0.0) * pltpu.roll(here, 1, 1)
        high, low = split(term)
        near = near + dot(high, hit[r], 1, 1) + dot(low, hit[r], 1, 1)
    point_diag[...] = jnp.sum(jnp.where(down == across, near, 0.0), axis=0, keepdims=True)
    tables = [near]
    ids_around = [value[1] for value in around]
    for d, r in ((0, cx - 1), (1, 0)):
        other = ids_around[d][r:r + 1, :].astype(jnp.int32)
        term = jnp.where(other == down, side2[d][r:r + 1, :], 0.0)
        high, low = split(term)
        tables.append(-(dot(high, hit[r], 1, 1) + dot(low, hit[r], 1, 1)))
    for d, q in ((2, cy - 1), (3, 0)):
        other = ids_around[d][:, q:q + 1].astype(jnp.int32)
        term = jnp.where(other == lane, side2[d][:, q:q + 1], 0.0)
        here = jnp.where(ids[:, q:q + 1] == lane, 1.0, 0.0)
        high, low = split(term)
        here = here.astype(BF16)
        tables.append(-(dot(high, here, 0, 0) + dot(low, here, 0, 0)))
    for i, table in enumerate(tables):
        high, low = split(table)
        big_hi[i] = high
        big_lo[i] = low

    tall = lax.broadcasted_iota(jnp.int32, (4 * cx, cy), 0) % cx

    def restrict_points(first, second):
        h0, l0 = split(first)
        h1, l1 = split(second)
        left = jnp.concatenate([h0, h1, l0, l1], axis=0)
        out = jnp.zeros((4 * cx, cy), F32)
        for r in range(cx):
            out = jnp.where(tall == r, dot(left, hit[r], 1, 1), out)
        parts = [jnp.sum(out[i * cx:(i + 1) * cx] + out[(i + 2) * cx:(i + 3) * cx], axis=0, keepdims=True)
                 for i in range(2)]
        return jnp.concatenate(parts, axis=0)

    point_cross[...] = restrict_points(cross2, cross2)

    inner = (diag2 - jnp.where(row < cx - 1, side2[0], 0.0) - jnp.where(row > 0, side2[1], 0.0)
             - jnp.where(lane < cy - 1, side2[2], 0.0) - jnp.where(lane > 0, side2[3], 0.0))
    entries = (inner, cross2, jnp.where(row == cx - 1, side2[0], 0.0), jnp.where(row == 0, side2[1], 0.0),
               jnp.where(last_lane, side2[2], 0.0), jnp.where(first_lane, side2[3], 0.0))
    eight = lax.broadcasted_iota(jnp.int32, (8, cy), 0)
    tile = jnp.zeros((8, cy), F32)
    for i, entry in enumerate(entries):
        tile = jnp.where(eight == i, total(entry), tile)
    gathers[2][0][...] = tile
    gather(2)
    block_row = lax.broadcasted_iota(jnp.int32, (count, cy), 0)

    def coarse_correction(left):
        sums = jnp.sum(left, axis=1, keepdims=True)
        gathers[0][0][...] = jnp.where(wide % 2 == 0, sums[0:1], sums[1:2])
        slot = lax.rem(fine.turn, 2)
        gather(0, slot)
        right = gathers[0][1][slot, :, 0, :]
        diag, crossed, east, west, north, south = (gathers[2][1][0, :, i, :] for i in range(6))
        answer = COARSE_WEIGHT * right / diag
        for _ in range(CSWEEPS - 1):
            applied = diag * answer + crossed * pltpu.roll(answer, 1, 1) - (
                east * pltpu.roll(answer, count - ny, 0) + west * pltpu.roll(answer, ny, 0)
                + north * pltpu.roll(answer, count - 1, 0) + south * pltpu.roll(answer, 1, 0))
            answer = answer + COARSE_WEIGHT * (right - applied) / diag
        found = []
        for at in (me, me + ny, me - ny, me + 1, me - 1):
            line = jnp.sum(jnp.where(block_row == at, answer, 0.0), axis=0, keepdims=True)
            found.append(jnp.concatenate([line[:, 0:1], line[:, 1:2]], axis=0))
        return found

    def point_exchange(p, x):
        x_out[p] = x
        q = lax.rem(p + fine.turn, 2)
        copies = [pltpu.make_async_remote_copy(
            src_ref=x_out.at[p], dst_ref=x_in.at[q, d ^ 1], send_sem=x_send.at[p, d],
            recv_sem=x_recv.at[q, d ^ 1], device_id=sides[d][1], device_id_type=MESH) for d in range(4)]
        swap_edges(copies)
        return [x] + [x_in[q, d] for d in range(4)]

    def point_apply(xs):
        out = point_cross[...] * jnp.concatenate([xs[0][1:2], xs[0][0:1]], axis=0)
        for i, x in enumerate(xs):
            high, low = split(x)
            out = out + dot(high, big_hi[i], 1, 0) + dot(low, big_hi[i], 1, 0) + dot(high, big_lo[i], 1, 0)
        return out

    def point_cycle(right):
        scale = POINT_WEIGHT / point_diag[...]
        x = right * scale
        x = x + (right - point_apply(point_exchange(0, x))) * scale
        xs = point_exchange(1, x)
        found = coarse_correction(right - point_apply(xs))
        xs = [x + y for x, y in zip(xs, found)]
        x = xs[0] + (right - point_apply(xs)) * scale
        return x + (right - point_apply(point_exchange(0, x))) * scale

    def into_points(level, p, comb, right):
        kept = []
        level.leftover(p, comb, right, lambda k, value: kept.append(value))
        x = point_cycle(restrict_points(kept[0][0], kept[0][1]))
        spread_out = jnp.stack([
            jnp.take_along_axis(jnp.broadcast_to(x[v:v + 1], (cx, cy)), ids, axis=1,
                                mode="promise_in_bounds") for v in range(2)])
        return lambda k: spread_out

    def into_level(coarser, deeper):
        def inner(level, p, comb, right):
            size = level.depth // coarser.depth
            held = []

            def emit(k, value):
                held.append(value)
                if len(held) == size:
                    coarser.right[k // size] = sum(held)
                    held.clear()

            level.leftover(p, comb, right, emit)
            coarser.cycle(lambda k: coarser.right[k], deeper)
            return lambda k: coarser.field[0, k // size, :, own, :]
        return inner

    into_column = into_level(column, into_points)
    into_middle = into_level(middle, into_column)

    for k in range(layers):
        basis[0, k] = forcing[:, k]

    def iteration(j, carry):
        fine.turn = j
        packed = fine.cycle(lambda k: basis[j, k], into_middle)
        comb = fine.exchange(0, packed)

        def emit(k, value):
            basis[j + 1, k] = value
            stored[j, k] = fine.field[0, k, :, own, :]

        fine.leftover(0, comb, lambda k: basis[j, k], emit)
        return carry

    lax.fori_loop(0, ITERS, iteration, 0)

    names = [(i, j) for i in range(ITERS + 1) for j in range(i, ITERS + 1)]
    sums = {name: jnp.zeros((cx, cy), F32) for name in names}
    for k in range(layers):
        chain = [basis[i, k] for i in range(ITERS + 1)]
        terms = [chain[j] - chain[j + 1] for j in range(ITERS)] + [chain[0]]
        for i, j in names:
            prod = terms[i] * terms[j]
            sums[i, j] = sums[i, j] + prod[0] + prod[1]
    line = reduce_all([total(sums[name]) for name in names])
    gram = {name: pick(line, at) for at, name in enumerate(names)}
    rows = [[gram[min(i, j), max(i, j)] for j in range(ITERS + 1)] for i in range(ITERS)]
    for a in range(ITERS):
        for i in range(a + 1, ITERS):
            share = rows[i][a] / rows[a][a]
            for c in range(a, ITERS + 1):
                rows[i][c] = rows[i][c] - share * rows[a][c]
    weights = [None] * ITERS
    for a in reversed(range(ITERS)):
        part = rows[a][ITERS]
        for c in range(a + 1, ITERS):
            part = part - rows[a][c] * weights[c]
        weights[a] = part / rows[a][a]
    for k in range(layers):
        out = weights[0] * stored[0, k]
        rest = forcing[:, k] - weights[0] * (basis[0, k] - basis[1, k])
        for j in range(1, ITERS):
            out = out + weights[j] * stored[j, k]
            rest = rest - weights[j] * (basis[j, k] - basis[j + 1, k])
        solution[:, k] = out
        residual[:, k] = rest


def solution(mesh):
    nx, ny = mesh.shape["gx"], mesh.shape["gy"]
    count = nx * ny

    def body(forcing, viscosity, spread, coupling, friction, mask, aggs):
        layers, cx, cy = forcing.shape[1:]
        dma = pltpu.SemaphoreType.DMA

        def vm(*shape, dtype=F32):
            return pltpu.VMEM(shape, dtype)

        def level(n):
            return (
                vm(2, n, 2, cx + 2 * TOP, cy), vm(2, 2, n, 2, cy), vm(2, 2, n, 2, cy),
                vm(2, cx, cy), vm(2, 2, cx, cy), dma((2, 4)), dma((2, 4)),
                vm(n, cx, cy), vm(n, cx, cy), vm(4, n, cx, cy), vm(cx, cy), vm(n, cx, cy), vm(n, cx, cy),
                vm(n, 2, cx, cy), vm(n, 2, cx, cy), vm(1, cy),
            )

        scratch = (
            (level(layers), level(layers // 2), level(1)),
            tuple(vm(n, layers, 2, cx, cy) for n in (ITERS + 1, ITERS)),
            (vm(cx, cy, cy, dtype=BF16), vm(5, cy, cy, dtype=BF16), vm(5, cy, cy, dtype=BF16),
             vm(1, cy), vm(2, cy)),
            (vm(2, 2, cy), vm(2, 4, 2, cy), dma((2, 4)), dma((2, 4))),
            tuple((vm(n, cy), vm(2, count, n, cy), dma(()), dma((2,))) for n in (1, 1, 8)),
        )
        flat, tree = jax.tree.flatten(scratch)

        def run(*refs):
            kernel(nx, ny, layers, cx, cy, *refs[:9], *jax.tree.unflatten(tree, refs[9:]))

        shape = jax.ShapeDtypeStruct(forcing.shape, F32)
        whole = pl.BlockSpec(memory_space=pltpu.VMEM)
        return tuple(pl.pallas_call(
            run,
            out_shape=(shape, shape),
            in_specs=[whole] * 7,
            out_specs=(whole, whole),
            scratch_shapes=flat,
            compiler_params=pltpu.CompilerParams(has_side_effects=True, vmem_limit_bytes=60 * 1024 * 1024),
        )(forcing, viscosity, spread, coupling, friction, mask, aggs))

    return jax.shard_map(
        body,
        mesh=mesh,
        in_specs=(
            P(None, None, "gx", "gy"),
            P(None, "gx", "gy"),
            P(None, "gx", "gy"),
            P("gx", "gy"),
            P("gx", "gy"),
            P("gx", "gy"),
            P("gx", "gy"),
        ),
        out_specs=(P(None, None, "gx", "gy"), P(None, None, "gx", "gy")),
        check_vma=False,
    )
```
